32 devices in a mesh: sample: 16 (over z, y, core), gene: 2 (over x).
Axes of the slice: x: 2, y: 2, z: 4, core: 2. Of those that a mesh axis runs over, the one named last changes fastest.
Arguments:
- block_values: bfloat16 [2048, 128, 128], P(('sample', 'gene')), may hold values from -0.1875 to 0.1875
- block_coords: int32 [2048, 2], P(('sample', 'gene')), may hold values from 0 to 127, as said below
- block_counts: int32 [32], P(('sample', 'gene')), may hold values from 13 to 64, as said below
- random_cols: bfloat16 [32768, 256], P(('gene', 'sample')), may hold values from -6 to 6
Outputs:
- basis: float32 [16384, 256], P(('sample', 'gene'))
- factor: float32 [256, 256], replicated
The draws below stay inside these ranges and needn't reach their ends.
Inputs may be any that keep to these rules, and one draw needn't show every extreme that they name: `block_coords`: column 0 is a row block 0 to 7, column 1 a column block 0 to 127; the pairs of one device's slots are all distinct. `block_counts`: some devices use all 64 slots in every draw.
All inputs are finite; a program needn't handle non-finite values.
Results may differ from the reference program's by a relative error of at most 0.0027.
Values may be sent and summed in bfloat16 or wider, within the bound.
No kernel may reach another device: no remote copies, remote signals or barrier semaphores. Data moves between devices by JAX's collectives and lax.ppermute only.
A program may use at most 128 MiB of HBM per device.

```python
import jax
import jax.numpy as jnp
from jax import lax

GENES = 32768
RANK = 256
BLOCK = 128
RB_DEV = 8
NB_DEV = 64
CB_DEV = 128
CELLS = 16384
NBLK = 2048
N_SAMPLE = 16
N_GENE = 2


def draw_block_coords(key, part):
    device_keys = jax.random.split(key, N_SAMPLE * N_GENE)

    def one_device(device_key):
        order = jax.random.permutation(device_key, RB_DEV * CB_DEV)[:NB_DEV]
        return jnp.stack([order // CB_DEV, order % CB_DEV], axis=1)
    return jax.vmap(one_device)(device_keys).reshape(NB_DEV * N_SAMPLE * N_GENE, 2).astype(jnp.int32)


def draw_block_counts(key, part):
    device_total = N_SAMPLE * N_GENE
    device_idx = jnp.arange(device_total, dtype=jnp.int32)
    sample_idx = device_idx // N_GENE
    lowest = max(NB_DEV // 3, 1)
    rising = lowest + (NB_DEV - lowest) * sample_idx // max(N_SAMPLE - 1, 1)
    jitter = jax.random.randint(key, (device_total,), 0, NB_DEV // 8 + 1)
    counts = jnp.maximum(rising - jitter, 1)
    counts = jnp.where(device_idx == 0, lowest - NB_DEV // 8, counts)
    counts = jnp.where(sample_idx == N_SAMPLE - 1, NB_DEV, counts)
    return counts.astype(jnp.int32)


def block_scale(stream_key, dims, pieces, low, largest):
    gain = 1.0
    for position, parts in pieces:
        heights = jax.random.uniform(jax.random.fold_in(jax.random.fold_in(stream_key, 6), position), (parts,), jnp.float32, low / len(pieces), largest / len(pieces))
        gain = gain * jnp.repeat(jnp.exp(heights), dims[position] // parts).reshape((-1,) + (1,) * (len(dims) - 1 - position))
    return gain


def bell_draw(rng, dims, deviation, reach, pieces=(), kind=jnp.bfloat16):
    loudness = block_scale(rng, dims, pieces, -0.22, 0.18) if pieces else 1.0
    entries = jax.random.normal(rng, dims, jnp.float32) * deviation * loudness
    return jnp.minimum(jnp.maximum(entries, -reach), reach).astype(kind)


def setup_inputs(seed: int = 0) -> dict:
    seeds = jax.random.split(jax.random.key(seed), 5)
    return {
        "block_values": bell_draw(seeds[0], (NBLK, BLOCK, BLOCK), (CELLS * NB_DEV // (RB_DEV * CB_DEV)) ** -0.5, 0.1875, ((0, 32),)),
        "block_coords": draw_block_coords(jax.random.fold_in(seeds[4], 71), 0),
        "block_counts": draw_block_counts(jax.random.fold_in(seeds[4], 71), 0),
        "random_cols": bell_draw(seeds[3], (GENES, RANK), 1.0, 6.0, ((0, 32),)),
    }


def device_layout(block_values, block_coords):
    shaped_values = block_values.reshape(N_SAMPLE * N_GENE, NB_DEV, BLOCK, BLOCK)
    shaped_coords = block_coords.reshape(N_SAMPLE * N_GENE, NB_DEV, 2)
    return (shaped_values, shaped_coords)

def forward_product(block_values, block_coords, block_counts, right_side):
    shaped_values, shaped_coords = device_layout(block_values, block_coords)
    row_span = RB_DEV * BLOCK
    col_span = CB_DEV * BLOCK

    def one_device(summed, item):
        device, dev_values, dev_coords, used = item
        sample_idx = device // N_GENE
        gene_idx = device % N_GENE
        right_part = lax.dynamic_slice_in_dim(right_side, (gene_idx * col_span).astype(jnp.int32), col_span, 0)
        right_part = right_part.reshape(CB_DEV, BLOCK, RANK)
        picked = right_part[dev_coords[:, 1]]
        products = jnp.einsum('nij,njk->nik', dev_values.astype(jnp.float32), picked.astype(jnp.float32), precision=lax.Precision.HIGHEST)
        alive_mask = (jnp.arange(NB_DEV, dtype=jnp.int32) < used).astype(jnp.float32)
        row_onehot = (dev_coords[:, 0][None, :] == jnp.arange(RB_DEV, dtype=jnp.int32)[:, None]).astype(jnp.float32) * alive_mask[None, :]
        term = jnp.einsum('rn,nik->rik', row_onehot, products, precision=lax.Precision.HIGHEST).reshape(row_span, RANK)
        offset = (sample_idx * row_span).astype(jnp.int32)
        before = lax.dynamic_slice_in_dim(summed, offset, row_span, 0)
        return (lax.dynamic_update_slice_in_dim(summed, before + term, offset, 0), None)
    devices_idx = jnp.arange(N_SAMPLE * N_GENE, dtype=jnp.int32)
    summed, unused = lax.scan(one_device, jnp.zeros((CELLS, RANK), jnp.float32), (devices_idx, shaped_values, shaped_coords, block_counts))
    return summed

def backward_product(block_values, block_coords, block_counts, left_side):
    shaped_values, shaped_coords = device_layout(block_values, block_coords)
    row_span = RB_DEV * BLOCK
    col_span = CB_DEV * BLOCK

    def one_device(summed, item):
        device, dev_values, dev_coords, used = item
        sample_idx = device // N_GENE
        gene_idx = device % N_GENE
        left_part = lax.dynamic_slice_in_dim(left_side, (sample_idx * row_span).astype(jnp.int32), row_span, 0)
        left_part = left_part.reshape(RB_DEV, BLOCK, RANK)
        picked = left_part[dev_coords[:, 0]]
        products = jnp.einsum('nij,nik->njk', dev_values.astype(jnp.float32), picked.astype(jnp.float32), precision=lax.Precision.HIGHEST)
        alive_mask = (jnp.arange(NB_DEV, dtype=jnp.int32) < used).astype(jnp.float32)
        col_onehot = (dev_coords[:, 1][None, :] == jnp.arange(CB_DEV, dtype=jnp.int32)[:, None]).astype(jnp.float32) * alive_mask[None, :]
        term = jnp.einsum('cn,njk->cjk', col_onehot, products, precision=lax.Precision.HIGHEST).reshape(col_span, RANK)
        offset = (gene_idx * col_span).astype(jnp.int32)
        before = lax.dynamic_slice_in_dim(summed, offset, col_span, 0)
        return (lax.dynamic_update_slice_in_dim(summed, before + term, offset, 0), None)
    devices_idx = jnp.arange(N_SAMPLE * N_GENE, dtype=jnp.int32)
    summed, unused = lax.scan(one_device, jnp.zeros((GENES, RANK), jnp.float32), (devices_idx, shaped_values, shaped_coords, block_counts))
    return summed

def orthonormal(sketch):
    gram = jnp.dot(sketch.T.astype(jnp.float32), sketch.astype(jnp.float32), precision=lax.Precision.HIGHEST, preferred_element_type=jnp.float32) / CELLS
    lower = jnp.linalg.cholesky(gram)
    basis = jax.scipy.linalg.solve_triangular(lower, sketch.T, lower=True).T
    return (basis, lower)

def reference(block_values, block_coords, block_counts, random_cols):
    sketch = forward_product(block_values, block_coords, block_counts, random_cols)
    first_basis, first_lower = orthonormal(sketch)
    loadings = backward_product(block_values, block_coords, block_counts, first_basis.astype(jnp.bfloat16))
    second_sketch = forward_product(block_values, block_coords, block_counts, loadings.astype(jnp.bfloat16))
    basis, second_lower = orthonormal(second_sketch)
    return (basis, second_lower.T)
```

```python
import functools

import jax
import jax.numpy as jnp
from jax import lax
from jax.experimental import pallas as pl
from jax.experimental.pallas import tpu as pltpu
from jax.sharding import PartitionSpec as P

RANK = 256
BLOCK = 128
RB_DEV = 8
HALF = RANK // 2
PANEL = 16
UNROLL = 8
F32, BF16 = jnp.float32, jnp.bfloat16
ANY = pl.BlockSpec(memory_space=pl.ANY)
SMEM = pl.BlockSpec(memory_space=pltpu.SMEM)
VMEM = pl.BlockSpec(memory_space=pltpu.VMEM)


def split3(value):
    high = value.astype(BF16)
    rest = value - high.astype(F32)
    middle = rest.astype(BF16)
    return high, middle, (rest - middle.astype(F32)).astype(BF16)


def factor_kernel(scale, gram_ref, upper_ref, inverse_ref, work):
    n = gram_ref.shape[0]
    row = lax.broadcasted_iota(jnp.int32, (n, n), 0)
    col = lax.broadcasted_iota(jnp.int32, (n, n), 1)
    work[:, :n] = gram_ref[...] * scale
    work[:, n:] = (row == col).astype(F32)
    sub = lax.broadcasted_iota(jnp.int32, (PANEL, 1), 0)
    lane = lax.broadcasted_iota(jnp.int32, (PANEL, n), 1)
    wide = 2 * n // BLOCK

    def panel(p, carry):
        start = pl.multiple_of(p * PANEL, PANEL)
        rows = work[pl.ds(start, PANEL), :]
        rolled = pltpu.roll(rows[:, :n], n - start, axis=1)
        cols = [jnp.broadcast_to(rolled[:, j : j + 1], (PANEL, BLOCK)) for j in range(PANEL)]
        for k in range(PANEL):
            pivot = jnp.broadcast_to(cols[k][k : k + 1, :], (PANEL, BLOCK))
            inv = lax.rsqrt(pivot)
            inv = inv * (1.5 - 0.5 * pivot * inv * inv)
            lower = cols[k] * inv
            below = jnp.where(sub > k, lower, 0.0)
            upper = jnp.broadcast_to(rows[k : k + 1, :], (PANEL, 2 * n)) * jnp.concatenate([inv] * wide, axis=1)
            rows = jnp.where(sub == k, upper, rows - jnp.concatenate([below] * wide, axis=1) * upper)
            for j in range(k + 1, PANEL):
                cols[j] = cols[j] - below * jnp.broadcast_to(lower[j : j + 1, :], (PANEL, BLOCK))
        work[pl.ds(start, PANEL), :] = rows
        w1, w2, w3 = split3(jnp.where(lane >= start + PANEL, rows[:, :n], 0.0))
        b1, b2, b3 = split3(rows)
        left = jnp.concatenate([w1, w1, w2, w2, w1, w3], axis=0)
        right = jnp.concatenate([b1, b2, b1, b2, b3, b1], axis=0)
        work[...] = work[...] - lax.dot_general(
            left, right, (((0,), (0,)), ((), ())), preferred_element_type=F32
        )
        return carry

    lax.fori_loop(0, n // PANEL, panel, 0)
    upper_ref[...] = jnp.where(col >= row, work[:, :n], 0.0)
    inverse_ref[...] = jnp.where(col <= row, work[:, n:], 0.0)


def factor(gram, cells):
    n = gram.shape[0]
    return pl.pallas_call(
        functools.partial(factor_kernel, 1.0 / cells),
        out_shape=[jax.ShapeDtypeStruct((n, n), F32)] * 2,
        in_specs=[VMEM],
        out_specs=[VMEM] * 2,
        scratch_shapes=[pltpu.VMEM((n, 2 * n), F32)],
        name="factor",
    )(gram)


def gram_of(rows_block):
    return jnp.dot(rows_block.T, rows_block, precision=lax.Precision.HIGHEST, preferred_element_type=F32)


class Grid:
    def __init__(self, n_sample):
        self.n, self.nz = n_sample, n_sample // 4
        self.core = [(s, s ^ 1) for s in range(n_sample)]
        self.swap = [(0, 1), (1, 0)]

    def z_of(self, s):
        return s // 4

    def along_y(self, keep):
        return [(s, s ^ 2) for s in range(self.n) if keep(self.z_of(s))]

    def up(self, keep):
        return [(s, s + 4) for s in range(self.n - 4) if keep(self.z_of(s))]

    def down(self, keep):
        return [(s, s - 4) for s in range(4, self.n) if keep(self.z_of(s))]


def gather_chips(grid, mine):
    nz = grid.nz
    move = functools.partial(lax.ppermute, axis_name="sample")
    found = [(0, 0, mine), (0, 1, move(mine, perm=grid.along_y(lambda z: True)))]
    rising = falling = mine
    for d in range(1, nz):
        rising = move(rising, perm=grid.up(lambda z: z >= d - 1))
        falling = move(falling, perm=grid.down(lambda z: z <= nz - d))
        found += [(-d, 0, rising), (d, 0, falling)]
        found += [
            (-d, 1, move(rising, perm=grid.along_y(lambda z: z >= d))),
            (d, 1, move(falling, perm=grid.along_y(lambda z: z <= nz - 1 - d))),
        ]
    return found


def position():
    s = lax.axis_index("sample")
    return s // 4, (s // 2) % 2, s % 2


def load_values(own_hbm, other_hbm, values, sems):
    slots = own_hbm.shape[0]
    copies = [
        pltpu.make_async_copy(own_hbm, values.at[pl.ds(0, slots)], sems.at[0]),
        pltpu.make_async_copy(other_hbm, values.at[pl.ds(slots, slots)], sems.at[1]),
    ]
    for copy in copies:
        copy.start()
    return copies


def forward_kernel(nz, where, flip, transposed, own_code, other_code, own_hbm, other_hbm, *refs):
    chunks = refs[: len(where)]
    keep_hbm, send_hbm, values, right, total, value_sems, chunk_sems, out_sems = refs[len(where) :]
    z, y, core = position()
    g = lax.axis_index("gene")
    slots = own_hbm.shape[0]
    per = chunks[0].shape[0]
    copies = load_values(own_hbm, other_hbm, values, value_sems)
    inside = []
    for i, (dz, dy) in enumerate(where):
        chip = (z + dz) * 2 + (y + dy) % 2
        valid = jnp.logical_and(z + dz >= 0, z + dz < nz)
        inside.append((valid, i, jnp.where(valid, chip, 0)))
    for valid, i, chip in inside:

        @pl.when(valid)
        def _():
            pltpu.make_async_copy(chunks[i], right.at[pl.ds(chip * per, per)], chunk_sems.at[i]).start()

    trash = 2 * RB_DEV
    total[...] = jnp.zeros_like(total)
    for copy in copies:
        copy.wait()
    for valid, i, chip in inside:

        @pl.when(valid)
        def _():
            pltpu.make_async_copy(chunks[i], right.at[pl.ds(chip * per, per)], chunk_sems.at[i]).wait()

    flipped = core * (per // 2) if flip else 0
    dims = (((1,), (1 if transposed else 0,)), ((), ()))
    for h, codes in enumerate((own_code, other_code)):

        def turn(t, carry):
            spots, terms = [], []
            for u in range(UNROLL):
                code = codes[t * UNROLL + u]
                r = code >> 16
                spots.append(jnp.where(r >= RB_DEV, trash, r + h * RB_DEV))
                c = (code & 0xFFFF) ^ flipped
                terms.append(
                    lax.dot_general(values[h * slots + t * UNROLL + u], right[c], dims, preferred_element_type=F32)
                )
            for spot, term in zip(spots, terms):
                total[spot] += term
            return carry

        lax.fori_loop(0, slots // UNROLL, turn, 0)
    quarter = RB_DEV // 2
    outs = []
    for h in range(2):
        for k, (out, gene) in enumerate(((keep_hbm, g), (send_hbm, 1 - g))):
            outs.append(
                pltpu.make_async_copy(
                    total.at[pl.ds(h * RB_DEV + gene * quarter, quarter)], out.at[h], out_sems.at[2 * h + k]
                )
            )
    for copy in outs:
        copy.start()
    for copy in outs:
        copy.wait()


def forward(grid, codes, values, found, flip, transposed):
    slots = values[0].shape[0]
    per = found[0][2].shape[0]
    quarter = RB_DEV // 2
    half = jax.ShapeDtypeStruct((2, quarter, BLOCK, HALF), F32)
    return pl.pallas_call(
        functools.partial(forward_kernel, grid.nz, [spot[:2] for spot in found], flip, transposed),
        out_shape=[half, half],
        in_specs=[SMEM, SMEM, ANY, ANY] + [ANY] * len(found),
        out_specs=[ANY, ANY],
        scratch_shapes=[
            pltpu.VMEM((2 * slots, BLOCK, BLOCK), BF16),
            pltpu.VMEM((2 * grid.nz * per, BLOCK, BLOCK), BF16),
            pltpu.VMEM((2 * RB_DEV + 1, BLOCK, HALF), F32),
            pltpu.SemaphoreType.DMA((2,)),
            pltpu.SemaphoreType.DMA((len(found),)),
            pltpu.SemaphoreType.DMA((4,)),
        ],
        name="forward",
    )(*codes, *values, *[chunk for _, _, chunk in found])


def backward_kernel(nz, where, own_code, other_code, own_hbm, other_hbm, near_hbm, far_hbm, *refs):
    keeps, sends = refs[: len(where)], refs[len(where) : 2 * len(where)]
    values, left, total, staged, value_sems, left_sems, keep_sems, send_sems = refs[2 * len(where) :]
    z, y, _ = position()
    g = lax.axis_index("gene")
    slots = own_hbm.shape[0]
    per = keeps[0].shape[0]
    trash = 2 * nz * per
    quarter = RB_DEV // 2
    copies = load_values(own_hbm, other_hbm, values, value_sems)
    for h in range(2):
        for k, (source, gene) in enumerate(((near_hbm, g), (far_hbm, 1 - g))):
            for j in range(quarter):
                copies.append(
                    pltpu.make_async_copy(
                        source.at[h, :, pl.ds(j * BLOCK, BLOCK)],
                        left.at[h * RB_DEV + gene * quarter + j],
                        left_sems.at[(2 * h + k) * quarter + j],
                    )
                )
    for copy in copies[2:]:
        copy.start()

    def clear(i, carry):
        total[pl.ds(i * 16, 16)] = jnp.zeros((16, HALF, BLOCK), F32)
        return carry

    lax.fori_loop(0, trash // 16, clear, 0)
    for copy in copies:
        copy.wait()
    for h, codes in enumerate((own_code, other_code)):

        def turn(t, carry):
            spots, terms = [], []
            for u in range(UNROLL):
                code = codes[t * UNROLL + u]
                r = code >> 16
                spots.append(jnp.where(r >= RB_DEV, trash, code & 0xFFFF))
                terms.append(
                    jnp.dot(
                        left[h * RB_DEV + (r & (RB_DEV - 1))],
                        values[h * slots + t * UNROLL + u],
                        preferred_element_type=F32,
                    )
                )
            for spot, term in zip(spots, terms):
                total[spot] += term
            return carry

        lax.fori_loop(0, slots // UNROLL, turn, 0)

    def each(act):
        for i, dz in enumerate(where):
            target = z + dz
            valid = jnp.logical_and(target >= 0, target < nz)
            safe = jnp.where(valid, target, 0)

            @pl.when(valid)
            def _():
                act(
                    pltpu.make_async_copy(
                        total.at[pl.ds((2 * safe + y) * per, per)], keeps[i], keep_sems.at[i]
                    ),
                    pltpu.make_async_copy(staged.at[pl.ds(safe * per, per)], sends[i], send_sems.at[i]),
                )

    def narrow(i, carry):
        source = (2 * (i // per) + 1 - y) * per + i % per
        staged[i] = total[source].astype(BF16)
        return carry

    lax.fori_loop(0, nz * per, narrow, 0)
    each(lambda keep, send: (keep.start(), send.start()))
    each(lambda keep, send: (keep.wait(), send.wait()))


def backward(grid, codes, values, near, far, per):
    slots = values[0].shape[0]
    nz = grid.nz
    where = [0] + [d for k in range(1, nz) for d in (k, -k)]
    shape = (per, HALF, BLOCK)
    outs = pl.pallas_call(
        functools.partial(backward_kernel, nz, where),
        out_shape=[jax.ShapeDtypeStruct(shape, F32)] * len(where) + [jax.ShapeDtypeStruct(shape, BF16)] * len(where),
        in_specs=[SMEM, SMEM] + [ANY] * 4,
        out_specs=[ANY] * (2 * len(where)),
        scratch_shapes=[
            pltpu.VMEM((2 * slots, BLOCK, BLOCK), BF16),
            pltpu.VMEM((2 * RB_DEV, HALF, BLOCK), BF16),
            pltpu.VMEM((2 * nz * per + 1, HALF, BLOCK), F32),
            pltpu.VMEM((nz * per, HALF, BLOCK), BF16),
            pltpu.SemaphoreType.DMA((2,)),
            pltpu.SemaphoreType.DMA((2 * RB_DEV,)),
            pltpu.SemaphoreType.DMA((len(where),)),
            pltpu.SemaphoreType.DMA((len(where),)),
        ],
        name="backward",
    )(*codes, *values, near, far)
    return dict(zip(where, outs[: len(where)])), dict(zip(where, outs[len(where) :]))


def scatter_chips(grid, keeps, sends):
    nz = grid.nz
    move = functools.partial(lax.ppermute, axis_name="sample")
    rising = falling = None
    for d in range(nz - 1, 0, -1):
        for sign in (1, -1):
            if sign == 1:
                inside = lambda z: z <= nz - 1 - d
                perm = grid.up(inside)
            else:
                inside = lambda z: z >= d
                perm = grid.down(inside)
            part = keeps[sign * d] + move(sends[sign * d], perm=grid.along_y(inside)).astype(F32)
            before = rising if sign == 1 else falling
            if before is not None:
                part = part + before.astype(F32)
            moved = move(part.astype(BF16), perm=perm)
            if sign == 1:
                rising = moved
            else:
                falling = moved
    mine = keeps[0] + move(sends[0], perm=grid.along_y(lambda z: True)).astype(F32)
    return (mine + rising.astype(F32) + falling.astype(F32)).astype(BF16)


def sum_gram(grid, gram):
    move = functools.partial(lax.ppermute, axis_name="sample")
    _, _, core = position()
    part = gram.shape[0] // 2
    mine = lax.dynamic_slice_in_dim(gram, core * part, part, 0)
    theirs = lax.dynamic_slice_in_dim(gram, (1 - core) * part, part, 0)
    total = mine + move(theirs, perm=grid.core)
    total = total + lax.ppermute(total, "gene", grid.swap)
    total = total + move(total, perm=grid.along_y(lambda z: True))
    step = 1
    while step < grid.nz:
        total = total + move(total, perm=[(s, s ^ (4 * step)) for s in range(grid.n)])
        step *= 2
    other = move(total, perm=grid.core)
    return jnp.where(core == 0, jnp.concatenate([total, other]), jnp.concatenate([other, total]))


def whole_rows(grid, keep, send):
    _, _, core = position()
    part = (keep + lax.ppermute(send, "gene", grid.swap)).reshape(2, -1, HALF)
    other = lax.ppermute(part[1], "sample", grid.core)
    return jnp.where(
        core == 0,
        jnp.concatenate([part[0], other], axis=1),
        jnp.concatenate([other, part[0]], axis=1),
    )


def chip_local(grid, block_values, block_coords, block_counts, random_cols):
    _, _, core = position()
    move = functools.partial(lax.ppermute, axis_name="sample")
    slot_count = block_values.shape[0]
    cells = RB_DEV * BLOCK * grid.n
    used = jnp.arange(slot_count, dtype=jnp.int32) < block_counts[0]
    code = jnp.where(used, block_coords[:, 0], RB_DEV) * 65536 + block_coords[:, 1]
    codes = (code, move(code, perm=grid.core))
    values = (block_values, move(block_values, perm=grid.core))

    mine = lax.dynamic_slice_in_dim(random_cols, core * HALF, HALF, 1)
    theirs = lax.dynamic_slice_in_dim(random_cols, (1 - core) * HALF, HALF, 1)
    right = jnp.concatenate([mine, move(theirs, perm=grid.core)]).reshape(-1, BLOCK, HALF)
    per = right.shape[0]
    found = gather_chips(grid, right)
    sketch = whole_rows(grid, *forward(grid, codes, values, found, True, False))
    _, inverse = factor(sum_gram(grid, gram_of(sketch)), cells)
    first = lax.dot_general(
        inverse, sketch, (((1,), (1,)), ((), ())), precision=lax.Precision.HIGHEST, preferred_element_type=F32
    ).astype(BF16)
    mine = lax.dynamic_slice_in_dim(first, core * HALF, HALF, 0)
    theirs = lax.dynamic_slice_in_dim(first, (1 - core) * HALF, HALF, 0)
    near = jnp.stack([mine, move(theirs, perm=grid.core)])
    far = lax.ppermute(near, "gene", grid.swap)
    loadings = scatter_chips(grid, *backward(grid, codes, values, near, far, per))
    found = gather_chips(grid, loadings)
    second = whole_rows(grid, *forward(grid, codes, values, found, False, True))
    upper, inverse = factor(sum_gram(grid, gram_of(second)), cells)
    basis = lax.dot_general(
        second, inverse, (((1,), (1,)), ((), ())), precision=lax.Precision.HIGHEST, preferred_element_type=F32
    )
    return basis, upper


def take_forward(block_values, block_coords, alive, right_full):
    right_blocks = right_full.reshape(-1, BLOCK, RANK)
    picked = jnp.take(right_blocks, block_coords[:, 1], axis=0)
    products = jnp.einsum("nij,njk->nik", block_values, picked, preferred_element_type=F32)
    summed = jnp.zeros((RB_DEV, BLOCK, RANK), F32).at[block_coords[:, 0]].add(products * alive)
    return summed.reshape(RB_DEV * BLOCK, RANK)


def take_backward(block_values, block_coords, alive, left_rows, span_blocks):
    picked = jnp.take(left_rows.reshape(RB_DEV, BLOCK, RANK), block_coords[:, 0], axis=0)
    products = jnp.einsum("nij,nik->njk", block_values, picked, preferred_element_type=F32)
    summed = jnp.zeros((span_blocks, BLOCK, RANK), F32).at[block_coords[:, 1]].add(products * alive)
    return summed.reshape(span_blocks * BLOCK, RANK)


def any_local(n_sample, block_values, block_coords, block_counts, random_cols):
    cells = RB_DEV * BLOCK * n_sample
    alive = (jnp.arange(block_values.shape[0], dtype=jnp.int32) < block_counts[0]).astype(F32)[:, None, None]

    def basis_of(partial):
        summed = lax.psum_scatter(partial, "gene", scatter_dimension=0, tiled=True)
        upper, inverse = factor(lax.psum(gram_of(summed), ("sample", "gene")), cells)
        return jnp.dot(summed, inverse.T, precision=lax.Precision.HIGHEST, preferred_element_type=F32), upper

    random_full = lax.all_gather(random_cols, "sample", axis=0, tiled=True)
    first, _ = basis_of(take_forward(block_values, block_coords, alive, random_full))
    whole = lax.all_gather(first.astype(BF16), "gene", axis=0, tiled=True)
    part = take_backward(block_values, block_coords, alive, whole, random_full.shape[0] // BLOCK)
    mine = lax.psum_scatter(part, "sample", scatter_dimension=0, tiled=True).astype(BF16)
    loadings = lax.all_gather(mine, "sample", axis=0, tiled=True)
    return basis_of(take_forward(block_values, block_coords, alive, loadings))


def cores_are_samples(mesh):
    n_sample, n_gene = mesh.devices.shape
    if n_gene != 2 or n_sample % 4:
        return False
    chip = [tuple(d.coords) for d in mesh.devices[:, 0]]
    return all(chip[s] == chip[s ^ 1] for s in range(n_sample))


def solution(mesh):
    n_sample = mesh.shape["sample"]
    if cores_are_samples(mesh):
        body = functools.partial(chip_local, Grid(n_sample))
    else:
        body = functools.partial(any_local, n_sample)
    return jax.shard_map(
        body,
        mesh=mesh,
        in_specs=(
            P(("sample", "gene"), None, None),
            P(("sample", "gene"), None),
            P(("sample", "gene")),
            P(("gene", "sample"), None),
        ),
        out_specs=(P(("sample", "gene"), None), P()),
        check_vma=False,
    )
```

```python
import functools

import jax
import jax.numpy as jnp
from jax import lax
from jax.experimental import pallas as pl
from jax.experimental.pallas import tpu as pltpu
from jax.sharding import PartitionSpec as P

RANK = 256
BLOCK = 128
RB_DEV = 8
HALF = RANK // 2
PANEL = 16
UNROLL = 8
F32, BF16 = jnp.float32, jnp.bfloat16
ANY = pl.BlockSpec(memory_space=pl.ANY)
SMEM = pl.BlockSpec(memory_space=pltpu.SMEM)
VMEM = pl.BlockSpec(memory_space=pltpu.VMEM)


def split3(value):
    high = value.astype(BF16)
    rest = value - high.astype(F32)
    middle = rest.astype(BF16)
    return high, middle, (rest - middle.astype(F32)).astype(BF16)


def factor_kernel(scale, gram_ref, upper_ref, inverse_ref, work):
    n = gram_ref.shape[0]
    row = lax.broadcasted_iota(jnp.int32, (n, n), 0)
    col = lax.broadcasted_iota(jnp.int32, (n, n), 1)
    work[:, :n] = gram_ref[...] * scale
    work[:, n:] = (row == col).astype(F32)
    sub = lax.broadcasted_iota(jnp.int32, (PANEL, 1), 0)
    lane = lax.broadcasted_iota(jnp.int32, (PANEL, n), 1)
    wide = 2 * n // BLOCK

    def panel(p, carry):
        start = pl.multiple_of(p * PANEL, PANEL)
        rows = work[pl.ds(start, PANEL), :]
        rolled = pltpu.roll(rows[:, :n], n - start, axis=1)
        cols = [jnp.broadcast_to(rolled[:, j : j + 1], (PANEL, BLOCK)) for j in range(PANEL)]
        for k in range(PANEL):
            pivot = jnp.broadcast_to(cols[k][k : k + 1, :], (PANEL, BLOCK))
            inv = lax.rsqrt(pivot)
            inv = inv * (1.5 - 0.5 * pivot * inv * inv)
            lower = cols[k] * inv
            below = jnp.where(sub > k, lower, 0.0)
            upper = jnp.broadcast_to(rows[k : k + 1, :], (PANEL, 2 * n)) * jnp.concatenate([inv] * wide, axis=1)
            rows = jnp.where(sub == k, upper, rows - jnp.concatenate([below] * wide, axis=1) * upper)
            for j in range(k + 1, PANEL):
                cols[j] = cols[j] - below * jnp.broadcast_to(lower[j : j + 1, :], (PANEL, BLOCK))
        work[pl.ds(start, PANEL), :] = rows
        w1, w2, w3 = split3(jnp.where(lane >= start + PANEL, rows[:, :n], 0.0))
        b1, b2, b3 = split3(rows)
        left = jnp.concatenate([w1, w1, w2, w2, w1, w3], axis=0)
        right = jnp.concatenate([b1, b2, b1, b2, b3, b1], axis=0)
        work[...] = work[...] - lax.dot_general(
            left, right, (((0,), (0,)), ((), ())), preferred_element_type=F32
        )
        return carry

    lax.fori_loop(0, n // PANEL, panel, 0)
    upper_ref[...] = jnp.where(col >= row, work[:, :n], 0.0)
    inverse_ref[...] = jnp.where(col <= row, work[:, n:], 0.0)


def factor(gram, cells):
    n = gram.shape[0]
    return pl.pallas_call(
        functools.partial(factor_kernel, 1.0 / cells),
        out_shape=[jax.ShapeDtypeStruct((n, n), F32)] * 2,
        in_specs=[VMEM],
        out_specs=[VMEM] * 2,
        scratch_shapes=[pltpu.VMEM((n, 2 * n), F32)],
        compiler_params=pltpu.CompilerParams(vmem_limit_bytes=4 << 20),
        name="factor",
    )(gram)


def gram_of(rows_block):
    return jnp.dot(rows_block.T, rows_block, precision=lax.Precision.HIGHEST, preferred_element_type=F32)


class Grid:
    def __init__(self, n_sample):
        self.n, self.nz = n_sample, n_sample // 4
        self.core = [(s, s ^ 1) for s in range(n_sample)]
        self.swap = [(0, 1), (1, 0)]

    def z_of(self, s):
        return s // 4

    def along_y(self, keep):
        return [(s, s ^ 2) for s in range(self.n) if keep(self.z_of(s))]

    def up(self, keep):
        return [(s, s + 4) for s in range(self.n - 4) if keep(self.z_of(s))]

    def down(self, keep):
        return [(s, s - 4) for s in range(4, self.n) if keep(self.z_of(s))]


def gather_chips(grid, mine):
    nz = grid.nz
    move = functools.partial(lax.ppermute, axis_name="sample")
    found = [(0, 0, mine), (0, 1, move(mine, perm=grid.along_y(lambda z: True)))]
    rising = falling = mine
    for d in range(1, nz):
        rising = move(rising, perm=grid.up(lambda z: z >= d - 1))
        falling = move(falling, perm=grid.down(lambda z: z <= nz - d))
        found += [(-d, 0, rising), (d, 0, falling)]
        found += [
            (-d, 1, move(rising, perm=grid.along_y(lambda z: z >= d))),
            (d, 1, move(falling, perm=grid.along_y(lambda z: z <= nz - 1 - d))),
        ]
    return found


def position():
    s = lax.axis_index("sample")
    return s // 4, (s // 2) % 2, s % 2


def load_values(own_hbm, other_hbm, values, sems):
    slots = own_hbm.shape[0]
    copies = [
        pltpu.make_async_copy(own_hbm, values.at[pl.ds(0, slots)], sems.at[0]),
        pltpu.make_async_copy(other_hbm, values.at[pl.ds(slots, slots)], sems.at[1]),
    ]
    for copy in copies:
        copy.start()
    return copies


def forward_kernel(nz, where, flip, transposed, own_code, other_code, own_hbm, other_hbm, *refs):
    chunks = refs[: len(where)]
    keep_hbm, send_hbm, values, right, total, value_sems, chunk_sems, out_sems = refs[len(where) :]
    z, y, core = position()
    g = lax.axis_index("gene")
    slots = own_hbm.shape[0]
    per = chunks[0].shape[0]
    copies = load_values(own_hbm, other_hbm, values, value_sems)
    inside = []
    for i, (dz, dy) in enumerate(where):
        chip = (z + dz) * 2 + (y + dy) % 2
        valid = jnp.logical_and(z + dz >= 0, z + dz < nz)
        inside.append((valid, i, jnp.where(valid, chip, 0)))
    for valid, i, chip in inside:

        @pl.when(valid)
        def _():
            pltpu.make_async_copy(chunks[i], right.at[pl.ds(chip * per, per)], chunk_sems.at[i]).start()

    trash = 2 * RB_DEV
    total[...] = jnp.zeros_like(total)
    for copy in copies:
        copy.wait()
    for valid, i, chip in inside:

        @pl.when(valid)
        def _():
            pltpu.make_async_copy(chunks[i], right.at[pl.ds(chip * per, per)], chunk_sems.at[i]).wait()

    flipped = core * (per // 2) if flip else 0
    dims = (((1,), (1 if transposed else 0,)), ((), ()))
    for h, codes in enumerate((own_code, other_code)):

        def turn(t, carry):
            spots, terms = [], []
            for u in range(UNROLL):
                code = codes[t * UNROLL + u]
                r = code >> 16
                spots.append(jnp.where(r >= RB_DEV, trash, r + h * RB_DEV))
                c = (code & 0xFFFF) ^ flipped
                terms.append(
                    lax.dot_general(values[h * slots + t * UNROLL + u], right[c], dims, preferred_element_type=F32)
                )
            for spot, term in zip(spots, terms):
                total[spot] += term
            return carry

        lax.fori_loop(0, slots // UNROLL, turn, 0)
    quarter = RB_DEV // 2
    outs = []
    for h in range(2):
        for k, (out, gene) in enumerate(((keep_hbm, g), (send_hbm, 1 - g))):
            outs.append(
                pltpu.make_async_copy(
                    total.at[pl.ds(h * RB_DEV + gene * quarter, quarter)], out.at[h], out_sems.at[2 * h + k]
                )
            )
    for copy in outs:
        copy.start()
    for copy in outs:
        copy.wait()


def forward(grid, codes, values, found, flip, transposed):
    slots = values[0].shape[0]
    per = found[0][2].shape[0]
    quarter = RB_DEV // 2
    half = jax.ShapeDtypeStruct((2, quarter, BLOCK, HALF), F32)
    return pl.pallas_call(
        functools.partial(forward_kernel, grid.nz, [spot[:2] for spot in found], flip, transposed),
        out_shape=[half, half],
        in_specs=[SMEM, SMEM, ANY, ANY] + [ANY] * len(found),
        out_specs=[ANY, ANY],
        scratch_shapes=[
            pltpu.VMEM((2 * slots, BLOCK, BLOCK), BF16),
            pltpu.VMEM((2 * grid.nz * per, BLOCK, BLOCK), BF16),
            pltpu.VMEM((2 * RB_DEV + 1, BLOCK, HALF), F32),
            pltpu.SemaphoreType.DMA((2,)),
            pltpu.SemaphoreType.DMA((len(found),)),
            pltpu.SemaphoreType.DMA((4,)),
        ],
        compiler_params=pltpu.CompilerParams(vmem_limit_bytes=12 << 20),
        name="forward",
    )(*codes, *values, *[chunk for _, _, chunk in found])


def backward_kernel(nz, where, own_code, other_code, own_hbm, other_hbm, near_hbm, far_hbm, *refs):
    keeps, sends = refs[: len(where)], refs[len(where) : 2 * len(where)]
    values, left, total, staged, value_sems, left_sems, keep_sems, send_sems = refs[2 * len(where) :]
    z, y, _ = position()
    g = lax.axis_index("gene")
    slots = own_hbm.shape[0]
    per = keeps[0].shape[0]
    trash = 2 * nz * per
    quarter = RB_DEV // 2
    copies = load_values(own_hbm, other_hbm, values, value_sems)
    for h in range(2):
        for k, (source, gene) in enumerate(((near_hbm, g), (far_hbm, 1 - g))):
            for j in range(quarter):
                copies.append(
                    pltpu.make_async_copy(
                        source.at[h, :, pl.ds(j * BLOCK, BLOCK)],
                        left.at[h * RB_DEV + gene * quarter + j],
                        left_sems.at[(2 * h + k) * quarter + j],
                    )
                )
    for copy in copies[2:]:
        copy.start()

    def clear(i, carry):
        total[pl.ds(i * 16, 16)] = jnp.zeros((16, HALF, BLOCK), F32)
        return carry

    lax.fori_loop(0, trash // 16, clear, 0)
    for copy in copies:
        copy.wait()
    for h, codes in enumerate((own_code, other_code)):

        def turn(t, carry):
            spots, terms = [], []
            for u in range(UNROLL):
                code = codes[t * UNROLL + u]
                r = code >> 16
                spots.append(jnp.where(r >= RB_DEV, trash, code & 0xFFFF))
                terms.append(
                    jnp.dot(
                        left[h * RB_DEV + (r & (RB_DEV - 1))],
                        values[h * slots + t * UNROLL + u],
                        preferred_element_type=F32,
                    )
                )
            for spot, term in zip(spots, terms):
                total[spot] += term
            return carry

        lax.fori_loop(0, slots // UNROLL, turn, 0)

    def each(act):
        for i, dz in enumerate(where):
            target = z + dz
            valid = jnp.logical_and(target >= 0, target < nz)
            safe = jnp.where(valid, target, 0)

            @pl.when(valid)
            def _():
                act(
                    pltpu.make_async_copy(
                        total.at[pl.ds((2 * safe + y) * per, per)], keeps[i], keep_sems.at[i]
                    ),
                    pltpu.make_async_copy(staged.at[pl.ds(safe * per, per)], sends[i], send_sems.at[i]),
                )

    def narrow(i, carry):
        source = (2 * (i // per) + 1 - y) * per + i % per
        staged[i] = total[source].astype(BF16)
        return carry

    lax.fori_loop(0, nz * per, narrow, 0)
    each(lambda keep, send: (keep.start(), send.start()))
    each(lambda keep, send: (keep.wait(), send.wait()))


def backward(grid, codes, values, near, far, per):
    slots = values[0].shape[0]
    nz = grid.nz
    where = [0] + [d for k in range(1, nz) for d in (k, -k)]
    shape = (per, HALF, BLOCK)
    outs = pl.pallas_call(
        functools.partial(backward_kernel, nz, where),
        out_shape=[jax.ShapeDtypeStruct(shape, F32)] * len(where) + [jax.ShapeDtypeStruct(shape, BF16)] * len(where),
        in_specs=[SMEM, SMEM] + [ANY] * 4,
        out_specs=[ANY] * (2 * len(where)),
        scratch_shapes=[
            pltpu.VMEM((2 * slots, BLOCK, BLOCK), BF16),
            pltpu.VMEM((2 * RB_DEV, HALF, BLOCK), BF16),
            pltpu.VMEM((2 * nz * per + 1, HALF, BLOCK), F32),
            pltpu.VMEM((nz * per, HALF, BLOCK), BF16),
            pltpu.SemaphoreType.DMA((2,)),
            pltpu.SemaphoreType.DMA((2 * RB_DEV,)),
            pltpu.SemaphoreType.DMA((len(where),)),
            pltpu.SemaphoreType.DMA((len(where),)),
        ],
        compiler_params=pltpu.CompilerParams(vmem_limit_bytes=20 << 20),
        name="backward",
    )(*codes, *values, near, far)
    return dict(zip(where, outs[: len(where)])), dict(zip(where, outs[len(where) :]))


def scatter_chips(grid, keeps, sends):
    nz = grid.nz
    move = functools.partial(lax.ppermute, axis_name="sample")
    rising = falling = None
    for d in range(nz - 1, 0, -1):
        for sign in (1, -1):
            if sign == 1:
                inside = lambda z: z <= nz - 1 - d
                perm = grid.up(inside)
            else:
                inside = lambda z: z >= d
                perm = grid.down(inside)
            part = keeps[sign * d] + move(sends[sign * d], perm=grid.along_y(inside)).astype(F32)
            before = rising if sign == 1 else falling
            if before is not None:
                part = part + before.astype(F32)
            moved = move(part.astype(BF16), perm=perm)
            if sign == 1:
                rising = moved
            else:
                falling = moved
    mine = keeps[0] + move(sends[0], perm=grid.along_y(lambda z: True)).astype(F32)
    return (mine + rising.astype(F32) + falling.astype(F32)).astype(BF16)


def sum_gram(grid, gram):
    move = functools.partial(lax.ppermute, axis_name="sample")
    _, _, core = position()
    part = gram.shape[0] // 2
    mine = lax.dynamic_slice_in_dim(gram, core * part, part, 0)
    theirs = lax.dynamic_slice_in_dim(gram, (1 - core) * part, part, 0)
    total = mine + move(theirs, perm=grid.core)
    total = total + lax.ppermute(total, "gene", grid.swap)
    total = total + move(total, perm=grid.along_y(lambda z: True))
    step = 1
    while step < grid.nz:
        total = total + move(total, perm=[(s, s ^ (4 * step)) for s in range(grid.n)])
        step *= 2
    other = move(total, perm=grid.core)
    return jnp.where(core == 0, jnp.concatenate([total, other]), jnp.concatenate([other, total]))


def whole_rows(grid, keep, send):
    _, _, core = position()
    part = (keep + lax.ppermute(send, "gene", grid.swap)).reshape(2, -1, HALF)
    other = lax.ppermute(part[1], "sample", grid.core)
    return jnp.where(
        core == 0,
        jnp.concatenate([part[0], other], axis=1),
        jnp.concatenate([other, part[0]], axis=1),
    )


def chip_local(grid, block_values, block_coords, block_counts, random_cols):
    _, _, core = position()
    move = functools.partial(lax.ppermute, axis_name="sample")
    slot_count = block_values.shape[0]
    cells = RB_DEV * BLOCK * grid.n
    used = jnp.arange(slot_count, dtype=jnp.int32) < block_counts[0]
    code = jnp.where(used, block_coords[:, 0], RB_DEV) * 65536 + block_coords[:, 1]
    codes = (code, move(code, perm=grid.core))
    values = (block_values, move(block_values, perm=grid.core))

    mine = lax.dynamic_slice_in_dim(random_cols, core * HALF, HALF, 1)
    theirs = lax.dynamic_slice_in_dim(random_cols, (1 - core) * HALF, HALF, 1)
    right = jnp.concatenate([mine, move(theirs, perm=grid.core)]).reshape(-1, BLOCK, HALF)
    per = right.shape[0]
    found = gather_chips(grid, right)
    sketch = whole_rows(grid, *forward(grid, codes, values, found, True, False))
    _, inverse = factor(sum_gram(grid, gram_of(sketch)), cells)
    first = lax.dot_general(
        inverse, sketch, (((1,), (1,)), ((), ())), precision=lax.Precision.HIGHEST, preferred_element_type=F32
    ).astype(BF16)
    mine = lax.dynamic_slice_in_dim(first, core * HALF, HALF, 0)
    theirs = lax.dynamic_slice_in_dim(first, (1 - core) * HALF, HALF, 0)
    near = jnp.stack([mine, move(theirs, perm=grid.core)])
    far = lax.ppermute(near, "gene", grid.swap)
    loadings = scatter_chips(grid, *backward(grid, codes, values, near, far, per))
    found = gather_chips(grid, loadings)
    second = whole_rows(grid, *forward(grid, codes, values, found, False, True))
    upper, inverse = factor(sum_gram(grid, gram_of(second)), cells)
    basis = lax.dot_general(
        second, inverse, (((1,), (1,)), ((), ())), precision=lax.Precision.HIGHEST, preferred_element_type=F32
    )
    return basis, upper


def take_forward(block_values, block_coords, alive, right_full):
    right_blocks = right_full.reshape(-1, BLOCK, RANK)
    picked = jnp.take(right_blocks, block_coords[:, 1], axis=0)
    products = jnp.einsum("nij,njk->nik", block_values, picked, preferred_element_type=F32)
    summed = jnp.zeros((RB_DEV, BLOCK, RANK), F32).at[block_coords[:, 0]].add(products * alive)
    return summed.reshape(RB_DEV * BLOCK, RANK)


def take_backward(block_values, block_coords, alive, left_rows, span_blocks):
    picked = jnp.take(left_rows.reshape(RB_DEV, BLOCK, RANK), block_coords[:, 0], axis=0)
    products = jnp.einsum("nij,nik->njk", block_values, picked, preferred_element_type=F32)
    summed = jnp.zeros((span_blocks, BLOCK, RANK), F32).at[block_coords[:, 1]].add(products * alive)
    return summed.reshape(span_blocks * BLOCK, RANK)


def any_local(n_sample, block_values, block_coords, block_counts, random_cols):
    cells = RB_DEV * BLOCK * n_sample
    alive = (jnp.arange(block_values.shape[0], dtype=jnp.int32) < block_counts[0]).astype(F32)[:, None, None]

    def basis_of(partial):
        summed = lax.psum_scatter(partial, "gene", scatter_dimension=0, tiled=True)
        upper, inverse = factor(lax.psum(gram_of(summed), ("sample", "gene")), cells)
        return jnp.dot(summed, inverse.T, precision=lax.Precision.HIGHEST, preferred_element_type=F32), upper

    random_full = lax.all_gather(random_cols, "sample", axis=0, tiled=True)
    first, _ = basis_of(take_forward(block_values, block_coords, alive, random_full))
    whole = lax.all_gather(first.astype(BF16), "gene", axis=0, tiled=True)
    part = take_backward(block_values, block_coords, alive, whole, random_full.shape[0] // BLOCK)
    mine = lax.psum_scatter(part, "sample", scatter_dimension=0, tiled=True).astype(BF16)
    loadings = lax.all_gather(mine, "sample", axis=0, tiled=True)
    return basis_of(take_forward(block_values, block_coords, alive, loadings))


def cores_are_samples(mesh):
    n_sample, n_gene = mesh.devices.shape
    if n_gene != 2 or n_sample % 4:
        return False
    chip = [tuple(d.coords) for d in mesh.devices[:, 0]]
    return all(chip[s] == chip[s ^ 1] for s in range(n_sample))


def solution(mesh):
    n_sample = mesh.shape["sample"]
    if cores_are_samples(mesh):
        body = functools.partial(chip_local, Grid(n_sample))
    else:
        body = functools.partial(any_local, n_sample)
    return jax.shard_map(
        body,
        mesh=mesh,
        in_specs=(
            P(("sample", "gene"), None, None),
            P(("sample", "gene"), None),
            P(("sample", "gene")),
            P(("gene", "sample"), None),
        ),
        out_specs=(P(("sample", "gene"), None), P()),
        check_vma=False,
    )
```
